512 devices in a mesh: seg: 512 (over z, x, y, core).
Axes of the slice: x: 4, y: 4, z: 16, core: 2. Of those that a mesh axis runs over, the one named last changes fastest.
Arguments:
- density: float32 [2, 196608, 256], P(None, 'seg'), may hold values from -6 to 6
- near_blocks: bfloat16 [3, 2, 196608, 384], P(None, None, 'seg'), may hold values from -0.21875 to 0.21875
- projection: bfloat16 [2, 98304, 384], P(None, 'seg'), may hold values from -0.21875 to 0.21875
- transfers: bfloat16 [5, 2, 98304, 192], P(None, None, 'seg'), may hold values from -0.3125 to 0.3125
- interpolation: bfloat16 [2, 196608, 192], P(None, 'seg'), may hold values from -0.3125 to 0.3125
- precondition: float32 [2, 196608], P(None, 'seg'), may hold values from 0.5 to 1.5
Outputs:
- result: float32 [2, 196608, 256], P(None, 'seg')
The draws below stay inside these ranges and needn't reach their ends.
All inputs are finite; a program needn't handle non-finite values.
Results may differ from the reference program's by a relative error of at most 0.007.
Values may be sent and summed in bfloat16 or wider, within the bound.
No kernel may reach another device: no remote copies, remote signals or barrier semaphores. Data moves between devices by JAX's collectives and lax.ppermute only.
A program may use at most 64 MiB of HBM per device.

```python
import jax
import jax.numpy as jnp
from jax import lax

C = 384
R = 192
ANG = 256
LEVELS = 5
SEGS = 512


def levels(stream_key, shape, shards, least, high):
    level = 1.0
    for axis_at, blocks in shards:
        steps = jax.random.uniform(jax.random.fold_in(jax.random.fold_in(stream_key, 6), axis_at), (blocks,), jnp.float32, least / len(shards), high / len(shards))
        level = level * jnp.repeat(jnp.exp(steps), shape[axis_at] // blocks).reshape((-1,) + (1,) * (len(shape) - 1 - axis_at))
    return level


def noise(own_key, dims, scale, reach, shards=(), kind=jnp.bfloat16):
    level = levels(own_key, dims, shards, -0.22, 0.18) if shards else 1.0
    result = jax.random.normal(own_key, dims, jnp.float32) * scale * level
    return jnp.minimum(jnp.maximum(result, -reach), reach).astype(kind)


def setup_inputs(seed: int = 0) -> dict:
    streams_of = jax.random.split(jax.random.key(seed), 7)
    density = noise(streams_of[0], (2, SEGS * C, ANG), 1.0, 6.0, ((1, 512),), jnp.float32)
    near_blocks = noise(streams_of[1], (3, 2, SEGS * C, C), (2 * C) ** -0.5, 0.21875, ((2, 512),))
    projection = noise(streams_of[2], (2, SEGS * R, C), (2 * C) ** -0.5, 0.21875, ((1, 512),))
    transfers = noise(streams_of[3], (LEVELS, 2, SEGS * R, R), (2 * R) ** -0.5, 0.3125, ((2, 512),))
    interpolation = noise(streams_of[4], (2, SEGS * C, R), (2 * R) ** -0.5, 0.3125, ((1, 512),))
    precondition = jnp.clip(0.5 + 1.0 * jax.random.uniform(streams_of[5], (2, SEGS * C), jnp.float32) ** levels(streams_of[5], (2, SEGS * C), ((1, 512),), -0.2, 0.2), 0.5, 1.5)
    return {"density": density, "near_blocks": near_blocks, "projection": projection, "transfers": transfers, "interpolation": interpolation, "precondition": precondition}


def matmul_f32(left, right):
    return jnp.dot(left, right, preferred_element_type=jnp.float32)


def complex_product(matrix, vector):
    real_part = matmul_f32(matrix[0], vector[0]) - matmul_f32(matrix[1], vector[1])
    imag_part = matmul_f32(matrix[0], vector[1]) + matmul_f32(matrix[1], vector[0])
    return jnp.stack([real_part, imag_part])


def paired_product(pair_items):
    return complex_product(pair_items[0], pair_items[1])


def reference(density, near_blocks, projection, transfers, interpolation, precondition):
    dens_low = density.astype(jnp.bfloat16).reshape(2, SEGS, C, ANG)
    before = jnp.moveaxis(jnp.roll(dens_low, 1, axis=1), 1, 0)
    after = jnp.moveaxis(jnp.roll(dens_low, -1, axis=1), 1, 0)
    own_rows = jnp.moveaxis(dens_low, 1, 0)
    near_tiles = jnp.moveaxis(near_blocks.reshape(3, 2, SEGS, C, C), 2, 0)
    proj_tiles = jnp.moveaxis(projection.reshape(2, SEGS, R, C), 1, 0)

    def per_segment(items):
        tiles, mine, prior, later, proj = items
        near_sum = complex_product(tiles[0], mine) + complex_product(tiles[1], prior)
        near_sum = near_sum + complex_product(tiles[2], later)
        return near_sum, complex_product(proj, mine)

    near, coeffs = lax.map(per_segment, (near_tiles, own_rows, before, after, proj_tiles))
    segment_ids = jnp.arange(SEGS, dtype=jnp.int32)
    half_rows = R // 2
    for level_no in range(LEVELS):
        rounded = coeffs.astype(jnp.bfloat16)
        partner = rounded[jnp.bitwise_xor(segment_ids, 2 ** level_no)]
        lower_half = (jnp.bitwise_and(jnp.right_shift(segment_ids, level_no), 1) == 0)[:, None, None, None]
        joined = jnp.where(
            lower_half,
            jnp.concatenate([rounded[:, :, :half_rows], partner[:, :, :half_rows]], axis=2),
            jnp.concatenate([partner[:, :, half_rows:], rounded[:, :, half_rows:]], axis=2),
        )
        level_tiles = jnp.moveaxis(transfers[level_no].reshape(2, SEGS, R, R), 1, 0)
        coeffs = lax.map(paired_product, (level_tiles, joined))
    interp_tiles = jnp.moveaxis(interpolation.reshape(2, SEGS, C, R), 1, 0)
    far = lax.map(paired_product, (interp_tiles, coeffs.astype(jnp.bfloat16)))
    total = jnp.moveaxis(near + far, 0, 1).reshape(2, SEGS * C, ANG)
    pre_real = precondition[0][:, None]
    pre_imag = precondition[1][:, None]
    return jnp.stack([pre_real * total[0] - pre_imag * total[1], pre_real * total[1] + pre_imag * total[0]])
```

```python
import jax
import jax.numpy as jnp
from jax import lax
from jax.experimental import pallas as pl
from jax.experimental.pallas import tpu as pltpu
from jax.sharding import PartitionSpec as P

VMEM = pl.BlockSpec(memory_space=pltpu.VMEM)
HBM = pl.BlockSpec(memory_space=pltpu.HBM)
F32 = jnp.float32
BF16 = jnp.bfloat16


def swapped(array, mask):
    return lax.ppermute(array, "seg", [(i, i ^ mask) for i in range(lax.axis_size("seg"))])


def swapped_across(array):
    size = lax.axis_size("seg")
    return lax.ppermute(array, "seg", [(i, (((i + 1) ^ 1) - 1) % size) for i in range(size)])


def held(array):
    return pltpu.with_memory_space_constraint(array, pltpu.VMEM)


def in_hbm(array):
    return pltpu.with_memory_space_constraint(array, pltpu.HBM)


def call(kernel, name, limit, out_shape, operands, in_specs=None, out_specs=None, scratch=()):
    return pl.pallas_call(
        kernel,
        out_shape=out_shape,
        in_specs=in_specs or [VMEM] * len(operands),
        out_specs=out_specs or jax.tree.map(lambda _: VMEM, out_shape),
        scratch_shapes=scratch,
        compiler_params=pltpu.CompilerParams(vmem_limit_bytes=limit << 20),
        name=name,
    )(*((in_hbm if in_specs else held)(a) for a in operands))


def dot(left, right):
    return jnp.dot(left, right, preferred_element_type=F32)


def bit_of(level):
    return jnp.bitwise_and(jnp.right_shift(lax.axis_index("seg"), level), 1)


def product(real, imag, vec_real, vec_imag):
    return (
        dot(real, vec_real) - dot(imag, vec_imag),
        dot(real, vec_imag) + dot(imag, vec_real),
    )


def store_halves(level, half, matrix, vec_real, vec_imag, keep, send):
    bit = bit_of(level)
    for target, which in ((send, 1 - bit), (keep, bit)):
        rows = pl.ds(pl.multiple_of(which * half, half), half)
        real, imag = product(matrix(0, rows), matrix(1, rows), vec_real, vec_imag)
        target[0] = real.astype(BF16)
        target[1] = imag.astype(BF16)


def join(level, half, keep, recv, joined):
    bit = bit_of(level)
    joined[:, pl.ds(pl.multiple_of(bit * half, half), half)] = keep[...]
    joined[:, pl.ds(pl.multiple_of((1 - bit) * half, half), half)] = recv[...]


def first_kernel(density, projection, transfers, low, keep, send, stage, dens_buf, proj_buf, sems):
    copies = [
        pltpu.make_async_copy(projection, proj_buf, sems.at[0]),
        pltpu.make_async_copy(density.at[0], dens_buf.at[0], sems.at[1]),
        pltpu.make_async_copy(density.at[1], dens_buf.at[1], sems.at[2]),
        pltpu.make_async_copy(transfers.at[0], stage, sems.at[3]),
    ]
    for copy in copies:
        copy.start()
    copies[1].wait()
    low[0] = dens_buf[0].astype(BF16)
    copies[2].wait()
    low[1] = dens_buf[1].astype(BF16)
    copies[0].wait()
    half = proj_buf.shape[1] // 2
    store_halves(0, half, lambda part, rows: proj_buf[part, rows], low[0], low[1], keep, send)
    copies[3].wait()


def level_kernel(level, keep, recv, transfers, keep_out, send_out, joined):
    half = keep.shape[1]
    join(level, half, keep, recv, joined)
    store_halves(
        level + 1,
        half,
        lambda part, rows: transfers[min(level, transfers.shape[0] - 1), part, rows],
        joined[0],
        joined[1],
        keep_out,
        send_out,
    )


def near_kernel(near_blocks, low, recv, interpolation, out, turned):
    for part in range(2):
        turned[part] = jnp.transpose(interpolation[part])
    odd = bit_of(0)
    beside = 2 - odd
    for vec, block, fresh in ((low, 0, True), (recv, beside, False)):
        real, imag = product(near_blocks[block, 0], near_blocks[block, 1], vec[0], vec[1])
        if fresh:
            out[0] = real
            out[1] = imag
        else:
            out[0] += real
            out[1] += imag


def far_near_kernel(near_blocks, recv, near, out):
    across = 1 + bit_of(0)
    real, imag = product(near_blocks[across, 0], near_blocks[across, 1], recv[0], recv[1])
    out[0] = near[0] + real
    out[1] = near[1] + imag


def last_kernel(level, keep, recv, transfers, interpolation, near, precondition, out, joined, result, sems):
    half = keep.shape[1]
    join(level, half, keep, recv, joined)
    real, imag = product(transfers[level, 0], transfers[level, 1], joined[0], joined[1])
    real, imag = real.astype(BF16), imag.astype(BF16)
    pre = jnp.transpose(precondition[...])
    rows = near.shape[1]
    parts = 3
    step = rows // parts
    copies = []
    for part in range(parts):
        span = pl.ds(part * step, step)
        far_real, far_imag = product(interpolation[0, span], interpolation[1, span], real, imag)
        total_real = near[0, span] + far_real
        total_imag = near[1, span] + far_imag
        pre_real = pre[part * step : (part + 1) * step, 0:1]
        pre_imag = pre[part * step : (part + 1) * step, 1:2]
        result[0, span] = pre_real * total_real - pre_imag * total_imag
        result[1, span] = pre_real * total_imag + pre_imag * total_real
        copy = pltpu.make_async_copy(result.at[:, span], out.at[:, span], sems.at[part])
        copy.start()
        copies.append(copy)
    for copy in copies:
        copy.wait()


def body(density, near_blocks, projection, transfers, interpolation, precondition):
    rows, angles = density.shape[1:]
    rank = projection.shape[1]
    half = rank // 2
    levels = transfers.shape[0]
    block = pltpu.VMEM((2, half, angles), BF16)
    whole = pltpu.VMEM((2, rows, angles), F32)
    low16 = pltpu.VMEM((2, rows, angles), BF16)
    low, keep, send, stage = call(
        first_kernel,
        "first",
        4,
        (low16, block, block, pltpu.VMEM((2, rank, rank), BF16)),
        (density, projection, transfers),
        in_specs=[HBM] * 3,
        scratch=[
            pltpu.VMEM(density.shape, F32),
            pltpu.VMEM(projection.shape, BF16),
            pltpu.SemaphoreType.DMA((4,)),
        ],
    )
    joined = pltpu.VMEM((2, rank, angles), BF16)
    transfers, near_blocks = held(transfers), held(near_blocks)
    for level in range(levels):
        recv = swapped(send, 1 << level)
        if level == 1:
            beside = swapped(low, 1)
        if level == 2:
            across = swapped_across(low)
            near, turned = call(
                near_kernel,
                "near",
                4,
                (whole, pltpu.VMEM((2, rows, rank), BF16)),
                (near_blocks, low, beside, jnp.swapaxes(interpolation, 1, 2)),
            )
        if level == 3:
            near = call(far_near_kernel, "near2", 4, whole, (near_blocks, across, near))
        if level == levels - 1:
            break
        keep, send = call(
            lambda *refs, level=level: level_kernel(level, *refs),
            f"level{level}",
            2,
            (block, block),
            (keep, recv, transfers if level else stage[None]),
            scratch=[joined],
        )
    return call(
        lambda *refs: last_kernel(levels - 1, *refs),
        "last",
        4,
        jax.ShapeDtypeStruct((2, rows, angles), F32),
        (keep, recv, transfers, turned, near, precondition),
        out_specs=HBM,
        scratch=[joined, pltpu.VMEM((2, rows, angles), F32), pltpu.SemaphoreType.DMA((3,))],
    )


def solution(mesh):
    placed = (
        P(None, "seg", None),
        P(None, None, "seg", None),
        P(None, "seg", None),
        P(None, None, "seg", None),
        P(None, "seg", None),
        P(None, "seg"),
    )
    return jax.shard_map(
        body, mesh=mesh, in_specs=placed, out_specs=P(None, "seg", None), check_vma=False
    )
```

```python
import jax
import jax.numpy as jnp
from jax import lax
from jax.experimental import pallas as pl
from jax.experimental.pallas import tpu as pltpu
from jax.sharding import PartitionSpec as P


VMEM = pl.BlockSpec(memory_space=pltpu.VMEM)
HBM = pl.BlockSpec(memory_space=pltpu.HBM)
ANY = pl.BlockSpec(memory_space=pl.ANY)
F32 = jnp.float32
BF16 = jnp.bfloat16


def swapped(array, mask):
    return lax.ppermute(array, "seg", [(i, i ^ mask) for i in range(lax.axis_size("seg"))])


def swapped_across(array):
    size = lax.axis_size("seg")
    return lax.ppermute(array, "seg", [(i, ((i + 1) ^ 1) - 1) for i in range(1, size - 1)])


def moved(array, source, target):
    return lax.ppermute(array, "seg", [(source, target)])


def groups_of_four(level):
    low, high = 1 << level, 2 << level
    firsts = [i for i in range(lax.axis_size("seg")) if not i & (low | high)]
    return [[i, i | low, i | high, i | low | high] for i in firsts]


def held(array):
    return pltpu.with_memory_space_constraint(array, pltpu.VMEM)


def in_hbm(array):
    return pltpu.with_memory_space_constraint(array, pltpu.HBM)


PLACE = {pltpu.HBM: in_hbm, pltpu.VMEM: held, pl.ANY: lambda array: array}


def call(kernel, limit, out_shape, operands, in_specs=None, out_specs=None, scratch=(), aliases={}):
    in_specs = in_specs or [VMEM] * len(operands)
    return pl.pallas_call(
        kernel,
        out_shape=out_shape,
        in_specs=in_specs,
        out_specs=out_specs or jax.tree.map(lambda _: VMEM, out_shape),
        scratch_shapes=scratch,
        input_output_aliases=aliases,
        compiler_params=pltpu.CompilerParams(vmem_limit_bytes=limit << 20),
    )(*(PLACE[spec.memory_space](a) for a, spec in zip(operands, in_specs)))


def dot(left, right):
    return jnp.dot(left, right, preferred_element_type=F32)


def bit_of(level):
    return jnp.bitwise_and(jnp.right_shift(lax.axis_index("seg"), level), 1)


def product(real, imag, vec_real, vec_imag):
    return (
        dot(real, vec_real) - dot(imag, vec_imag),
        dot(real, vec_imag) + dot(imag, vec_real),
    )


def store_halves(level, half, matrix, vec_real, vec_imag, keep, send):
    bit = bit_of(level)
    for target, which in ((send, 1 - bit), (keep, bit)):
        rows = pl.ds(pl.multiple_of(which * half, half), half)
        real, imag = product(matrix(0, rows), matrix(1, rows), vec_real, vec_imag)
        target[0] = real.astype(BF16)
        target[1] = imag.astype(BF16)


def join(level, half, keep, recv, joined):
    bit = bit_of(level)
    joined[:, pl.ds(pl.multiple_of(bit * half, half), half)] = keep[...]
    joined[:, pl.ds(pl.multiple_of((1 - bit) * half, half), half)] = recv[...]


def half_rows(which, half):
    return pl.ds(pl.multiple_of(which * half, half), half)


def first_kernel(
    density,
    projection,
    transfers,
    low,
    keep,
    send,
    matrix0,
    matrix1,
    matrix2,
    dens_buf,
    proj_buf,
    sems,
):
    half = proj_buf.shape[1] // 2
    copies = [
        pltpu.make_async_copy(projection, proj_buf, sems.at[0]),
        pltpu.make_async_copy(density.at[0], dens_buf.at[0], sems.at[1]),
        pltpu.make_async_copy(density.at[1], dens_buf.at[1], sems.at[2]),
        pltpu.make_async_copy(transfers.at[0], matrix0.at[:, 0 : 2 * half], sems.at[3]),
        pltpu.make_async_copy(transfers.at[1], matrix1, sems.at[4]),
        pltpu.make_async_copy(transfers.at[2], matrix2, sems.at[5]),
        pltpu.make_async_copy(transfers.at[3, :, half_rows(1 - bit_of(4), half)], matrix0.at[:, 2 * half :], sems.at[6]),
    ]
    for copy in copies:
        copy.start()
    copies[1].wait()
    low[0] = dens_buf[0].astype(BF16)
    copies[2].wait()
    low[1] = dens_buf[1].astype(BF16)
    copies[0].wait()
    store_halves(0, half, lambda part, rows: proj_buf[part, rows], low[0], low[1], keep, send)
    for copy in copies[3:]:
        copy.wait()


def level_kernel(level, keep, recv, matrix, keep_out, send_out, joined):
    half = keep.shape[1]
    join(level, half, keep, recv, joined)
    store_halves(
        level + 1, half, lambda part, rows: matrix[part, rows], joined[0], joined[1], keep_out, send_out
    )


def level0_kernel(keep, recv, matrix, keep_out, send_out, rows3, joined):
    level_kernel(0, keep, recv, matrix, keep_out, send_out, joined)
    rows3[...] = matrix[:, matrix.shape[2] :]


def spread_kernel(level, keep, recv, matrix, out, joined, result, sems):
    half = keep.shape[1]
    join(level, half, keep, recv, joined)
    copies = []
    for which in range(2):
        rows = pl.ds(which * half, half)
        real, imag = product(matrix[0, rows], matrix[1, rows], joined[0], joined[1])
        result[which, 0] = real.astype(BF16)
        result[which, 1] = imag.astype(BF16)
        for member in (which, which + 2):
            copy = pltpu.make_async_copy(result.at[which], out.at[member], sems.at[member])
            copy.start()
            copies.append(copy)
    for copy in copies:
        copy.wait()


def join_four(level, recv, rows_own, rows_other, pair, joined):
    half = recv.shape[2]
    bit = bit_of(level + 1)
    pair[bit] = rows_own[...]
    pair[1 - bit] = rows_other[...]
    for side in range(2):
        vecs = [
            jnp.concatenate([recv[2 * side, part], recv[2 * side + 1, part]]) for part in range(2)
        ]
        real, imag = product(pair[side, 0], pair[side, 1], *vecs)
        joined[0, pl.ds(side * half, half)] = real.astype(BF16)
        joined[1, pl.ds(side * half, half)] = imag.astype(BF16)


def near_kernel(here, *refs):
    @pl.when((lax.axis_index("seg") == 0) == here)
    def _():
        near_work(here, *refs)


def near_work(
    here,
    near_blocks,
    interpolation,
    transfers,
    precondition,
    low,
    beside,
    across,
    *refs,
):
    out, turned, own3, matrix4, scales, buf, flat, vec_buf, sems = refs[-9:]
    half = own3.shape[1]
    odd = bit_of(0)
    order = ((0, low), (2 - odd, beside), (1 + odd, vec_buf if here else across))
    copies = [
        pltpu.make_async_copy(near_blocks.at[block], buf.at[i], sems.at[i])
        for i, (block, _) in enumerate(order)
    ]
    copies += [
        pltpu.make_async_copy(interpolation, flat, sems.at[3]),
        pltpu.make_async_copy(transfers.at[3, :, half_rows(bit_of(4), half)], own3, sems.at[4]),
        pltpu.make_async_copy(transfers.at[4], matrix4, sems.at[5]),
        pltpu.make_async_copy(precondition, scales, sems.at[6]),
    ]
    if here:
        copies.append(pltpu.make_async_copy(across, vec_buf, sems.at[7]))
    for copy in copies:
        copy.start()
    for i, (_, vec) in enumerate(order):
        copies[i].wait()
        if i == 2 and here:
            copies[7].wait()
        real, imag = product(buf[i, 0], buf[i, 1], vec[0], vec[1])
        if i:
            out[0] += real
            out[1] += imag
        else:
            out[0] = real
            out[1] = imag
    for copy in copies[3:7]:
        copy.wait()
    for part in range(2):
        turned[part] = jnp.transpose(flat[part])


def weighted(pre, real, imag):
    return pre[:, 0:1] * real - pre[:, 1:2] * imag, pre[:, 0:1] * imag + pre[:, 1:2] * real


def at_final():
    return lax.axis_index("seg") == lax.axis_size("seg") - 1


def finish_kernel(out_before, result, block, precondition, from_first, out, buf, sems):
    @pl.when(at_final())
    def _():
        pre = jnp.transpose(precondition[...])
        copies = []
        for part, span in enumerate(parts_of(result.shape[1])):
            real, imag = product(block[0, span], block[1, span], from_first[0], from_first[1])
            real, imag = weighted(pre[span], real, imag)
            buf[0, span] = result[0, span] + real
            buf[1, span] = result[1, span] + imag
            copy = pltpu.make_async_copy(buf.at[:, span], out.at[:, span], sems.at[part])
            copy.start()
            copies.append(copy)
        for copy in copies:
            copy.wait()


def parts_of(rows):
    step = rows // 3
    return [slice(part * step, (part + 1) * step) for part in range(3)]


def last_kernel(
    level,
    near_blocks,
    recv,
    rows_own,
    rows_other,
    matrix,
    interpolation,
    near,
    precondition,
    out,
    result,
    block,
    pair,
    joined,
    sems,
):
    fetch = pltpu.make_async_copy(near_blocks.at[2], block, sems.at[3])
    pl.when(at_final())(fetch.start)
    pre = jnp.transpose(precondition[...])
    join_four(level - 1, recv, rows_own, rows_other, pair, joined)
    real, imag = product(matrix[0], matrix[1], joined[0], joined[1])
    real, imag = real.astype(BF16), imag.astype(BF16)
    copies = []
    for part, span in enumerate(parts_of(near.shape[1])):
        far_real, far_imag = product(interpolation[0, span], interpolation[1, span], real, imag)
        result[0, span], result[1, span] = weighted(
            pre[span], near[0, span] + far_real, near[1, span] + far_imag
        )
        copy = pltpu.make_async_copy(result.at[:, span], out.at[:, span], sems.at[part])
        copy.start()
        copies.append(copy)
    for copy in copies:
        copy.wait()
    pl.when(at_final())(fetch.wait)


def body(density, near_blocks, projection, transfers, interpolation, precondition):
    rows, angles = density.shape[1:]
    rank = projection.shape[1]
    half = rank // 2
    levels = transfers.shape[0]
    block = pltpu.VMEM((2, half, angles), BF16)
    whole = pltpu.VMEM((2, rows, angles), F32)
    low16 = pltpu.VMEM((2, rows, angles), BF16)
    square = pltpu.VMEM((2, rank, rank), BF16)
    rows_half = pltpu.VMEM((2, half, rank), BF16)
    low, keep, send, matrix0, matrix1, matrix2 = call(
        first_kernel,
        4,
        (
            low16,
            block,
            block,
            pltpu.VMEM((2, rank + half, rank), BF16),
            square,
            square,
        ),
        (density, projection, transfers),
        in_specs=[HBM] * 3,
        scratch=[
            pltpu.VMEM(density.shape, F32),
            pltpu.VMEM(projection.shape, BF16),
            pltpu.SemaphoreType.DMA((7,)),
        ],
    )
    joined = pltpu.VMEM((2, rank, angles), BF16)
    pair = pltpu.VMEM((2, 2, half, rank), BF16)
    recv = swapped(send, 1)
    keep, send, rows3 = call(
        level0_kernel, 2, (block, block, rows_half), (keep, recv, matrix0), scratch=[joined]
    )
    recv = swapped(send, 2)
    keep, send = call(
        lambda *refs: level_kernel(1, *refs),
        2,
        (block, block),
        (keep, recv, matrix1),
        scratch=[joined],
    )
    recv = swapped(send, 4)
    rows3 = swapped(rows3, 16)
    beside = swapped(low, 1)
    across = swapped_across(low)
    final = lax.axis_size("seg") - 1
    from_final = moved(low, final, 0)
    from_first = moved(low, 0, final)
    send = call(
        lambda *refs: spread_kernel(2, *refs),
        2,
        jax.ShapeDtypeStruct((4, 2, half, angles), BF16),
        (keep, recv, matrix2),
        out_specs=HBM,
        scratch=[
            joined,
            pltpu.VMEM((2, 2, half, angles), BF16),
            pltpu.SemaphoreType.DMA((4,)),
        ],
    )
    recv = lax.all_to_all(send, "seg", 0, 0, axis_index_groups=groups_of_four(3))
    work = (whole, pltpu.VMEM((2, rows, rank), BF16), rows_half, square, pltpu.VMEM((2, rows), F32))
    done = ()
    for here in (True, False):
        done = call(
            lambda *refs, here=here: near_kernel(here, *refs),
            6,
            work,
            (
                near_blocks,
                jnp.swapaxes(interpolation, 1, 2),
                transfers,
                precondition,
                low,
                beside,
                from_final if here else across,
                *done,
            ),
            in_specs=[HBM] * 4 + [VMEM] * 2 + [ANY if here else VMEM] + [VMEM] * len(done),
            scratch=[
                pltpu.VMEM(near_blocks.shape, BF16),
                pltpu.VMEM((2, rank, rows), BF16),
                pltpu.VMEM(low.shape, BF16),
                pltpu.SemaphoreType.DMA((8,)),
            ],
            aliases={7 + k: k for k in range(len(done))},
        )
    near, turned, own3, matrix4, scales = done
    out = jax.ShapeDtypeStruct((2, rows, angles), F32)
    out, result, last_block = call(
        lambda *refs: last_kernel(levels - 1, *refs),
        6,
        (out, whole, pltpu.VMEM(near_blocks.shape[1:], BF16)),
        (near_blocks, recv, own3, rows3, matrix4, turned, near, scales),
        in_specs=[HBM] + [VMEM] * 7,
        out_specs=[HBM, VMEM, VMEM],
        scratch=[pair, joined, pltpu.SemaphoreType.DMA((4,))],
    )
    return call(
        finish_kernel,
        4,
        jax.ShapeDtypeStruct((2, rows, angles), F32),
        (out, result, last_block, scales, from_first),
        in_specs=[HBM] + [VMEM] * 4,
        out_specs=HBM,
        scratch=[pltpu.VMEM((2, rows, angles), F32), pltpu.SemaphoreType.DMA((3,))],
        aliases={0: 0},
    )


def solution(mesh):
    placed = (
        P(None, "seg", None),
        P(None, None, "seg", None),
        P(None, "seg", None),
        P(None, None, "seg", None),
        P(None, "seg", None),
        P(None, "seg"),
    )

    return jax.shard_map(
        body, mesh=mesh, in_specs=placed, out_specs=P(None, "seg", None), check_vma=False
    )
```

```python
import jax
import jax.numpy as jnp
from jax import lax
from jax.experimental import pallas as pl
from jax.experimental.pallas import tpu as pltpu
from jax.sharding import PartitionSpec as P


VMEM = pl.BlockSpec(memory_space=pltpu.VMEM)
HBM = pl.BlockSpec(memory_space=pltpu.HBM)
ANY = pl.BlockSpec(memory_space=pl.ANY)
F32 = jnp.float32
BF16 = jnp.bfloat16


def swapped(array, mask):
    return lax.ppermute(array, "seg", [(i, i ^ mask) for i in range(lax.axis_size("seg"))])


def swapped_across(array):
    size = lax.axis_size("seg")
    return lax.ppermute(array, "seg", [(i, ((i + 1) ^ 1) - 1) for i in range(1, size - 1)])


def moved(array, source, target):
    return lax.ppermute(array, "seg", [(source, target)])


def groups_of_four(level):
    low, high = 1 << level, 2 << level
    firsts = [i for i in range(lax.axis_size("seg")) if not i & (low | high)]
    return [[i, i | low, i | high, i | low | high] for i in firsts]


def held(array):
    return pltpu.with_memory_space_constraint(array, pltpu.VMEM)


def in_hbm(array):
    return pltpu.with_memory_space_constraint(array, pltpu.HBM)


PLACE = {pltpu.HBM: in_hbm, pltpu.VMEM: held, pl.ANY: lambda array: array}


def call(kernel, limit, out_shape, operands, in_specs=None, out_specs=None, scratch=(), aliases={}):
    in_specs = in_specs or [VMEM] * len(operands)
    return pl.pallas_call(
        kernel,
        out_shape=out_shape,
        in_specs=in_specs,
        out_specs=out_specs or jax.tree.map(lambda _: VMEM, out_shape),
        scratch_shapes=scratch,
        input_output_aliases=aliases,
        compiler_params=pltpu.CompilerParams(vmem_limit_bytes=limit << 20),
    )(*(PLACE[spec.memory_space](a) for a, spec in zip(operands, in_specs)))


def dot(left, right):
    return jnp.dot(left, right, preferred_element_type=F32)


def bit_of(level):
    return jnp.bitwise_and(jnp.right_shift(lax.axis_index("seg"), level), 1)


def product(real, imag, vec_real, vec_imag):
    return (
        dot(real, vec_real) - dot(imag, vec_imag),
        dot(real, vec_imag) + dot(imag, vec_real),
    )


def store_halves(level, half, matrix, vec_real, vec_imag, keep, send):
    bit = bit_of(level)
    for target, which in ((send, 1 - bit), (keep, bit)):
        rows = pl.ds(pl.multiple_of(which * half, half), half)
        real, imag = product(matrix(0, rows), matrix(1, rows), vec_real, vec_imag)
        target[0] = real.astype(BF16)
        target[1] = imag.astype(BF16)


def join(level, half, keep, recv, joined):
    bit = bit_of(level)
    joined[:, pl.ds(pl.multiple_of(bit * half, half), half)] = keep[...]
    joined[:, pl.ds(pl.multiple_of((1 - bit) * half, half), half)] = recv[...]


def half_rows(which, half):
    return pl.ds(pl.multiple_of(which * half, half), half)


def first_kernel(
    density,
    projection,
    transfers,
    low,
    keep,
    packed,
    matrix0,
    matrix1,
    matrix2,
    dens_buf,
    proj_buf,
    sems,
):
    half = proj_buf.shape[1] // 2
    copies = [
        pltpu.make_async_copy(projection, proj_buf, sems.at[0]),
        pltpu.make_async_copy(density.at[0], dens_buf.at[0], sems.at[1]),
        pltpu.make_async_copy(density.at[1], dens_buf.at[1], sems.at[2]),
        pltpu.make_async_copy(transfers.at[0], matrix0.at[:, 0 : 2 * half], sems.at[3]),
        pltpu.make_async_copy(transfers.at[1], matrix1, sems.at[4]),
        pltpu.make_async_copy(transfers.at[2], matrix2, sems.at[5]),
        pltpu.make_async_copy(transfers.at[3, :, half_rows(1 - bit_of(4), half)], matrix0.at[:, 2 * half :], sems.at[6]),
    ]
    for k in (1, 2, 0, 3, 4, 5, 6):
        copies[k].start()
    for part in range(2):
        copies[part + 1].wait()
        low[part] = dens_buf[part].astype(BF16)
        packed[part, half:] = low[part]
    copies[0].wait()
    store_halves(
        0,
        half,
        lambda part, rows: proj_buf[part, rows],
        low[0],
        low[1],
        keep,
        packed.at[:, 0:half],
    )
    for copy in copies[3:]:
        copy.wait()


def level_kernel(level, keep, recv, matrix, keep_out, send_out, joined):
    half = keep.shape[1]
    join(level, half, keep, recv, joined)
    store_halves(
        level + 1, half, lambda part, rows: matrix[part, rows], joined[0], joined[1], keep_out, send_out
    )


def level0_kernel(keep, recv, matrix, keep_out, send_out, rows3, joined):
    half = keep.shape[1]
    level_kernel(0, keep, recv.at[:, 0:half], matrix, keep_out, send_out, joined)
    rows3[...] = matrix[:, matrix.shape[2] :]


def spread_kernel(level, keep, recv, matrix, out, joined, result, sems):
    half = keep.shape[1]
    join(level, half, keep, recv, joined)
    copies = []
    for which in range(2):
        rows = pl.ds(which * half, half)
        real, imag = product(matrix[0, rows], matrix[1, rows], joined[0], joined[1])
        result[which, 0] = real.astype(BF16)
        result[which, 1] = imag.astype(BF16)
        for member in (which, which + 2):
            copy = pltpu.make_async_copy(result.at[which], out.at[member], sems.at[member])
            copy.start()
            copies.append(copy)
    for copy in copies:
        copy.wait()


def join_four(recv, pair, joined):
    half = recv.shape[2]
    for side in range(2):
        vecs = [
            jnp.concatenate([recv[2 * side, part], recv[2 * side + 1, part]]) for part in range(2)
        ]
        real, imag = product(pair[side, 0], pair[side, 1], *vecs)
        joined[0, pl.ds(side * half, half)] = real.astype(BF16)
        joined[1, pl.ds(side * half, half)] = imag.astype(BF16)


def near_kernel(here, *refs):
    @pl.when((lax.axis_index("seg") == 0) == here)
    def _():
        near_work(*refs)


def near_work(
    near_blocks,
    interpolation,
    transfers,
    precondition,
    low,
    beside,
    rows3,
    across,
    *refs,
):
    out, turned, pair, matrix4, scales, buf, flat, vec_buf, sems = refs[-9:]
    half = pair.shape[2]
    side = bit_of(4)
    beside = beside.at[:, half:]
    odd = bit_of(0)
    order = ((0, low), (2 - odd, beside), (1 + odd, vec_buf))
    copies = [
        pltpu.make_async_copy(near_blocks.at[block], buf.at[i], sems.at[i])
        for i, (block, _) in enumerate(order)
    ]
    copies += [
        pltpu.make_async_copy(interpolation, flat, sems.at[3]),
        pltpu.make_async_copy(transfers.at[3, :, half_rows(side, half)], pair.at[side], sems.at[4]),
        pltpu.make_async_copy(rows3, pair.at[1 - side], sems.at[7]),
        pltpu.make_async_copy(transfers.at[4], matrix4, sems.at[5]),
        pltpu.make_async_copy(precondition, scales, sems.at[6]),
    ]
    copies.append(pltpu.make_async_copy(across, vec_buf, sems.at[8]))
    for copy in copies:
        copy.start()
    for i, (_, vec) in enumerate(order):
        copies[i].wait()
        if i == 2:
            copies[8].wait()
        real, imag = product(buf[i, 0], buf[i, 1], vec[0], vec[1])
        if i:
            out[0] += real
            out[1] += imag
        else:
            out[0] = real
            out[1] = imag
    for copy in copies[3:8]:
        copy.wait()
    for part in range(2):
        turned[part] = jnp.transpose(flat[part])


def weighted(pre, real, imag):
    return pre[:, 0:1] * real - pre[:, 1:2] * imag, pre[:, 0:1] * imag + pre[:, 1:2] * real


def at_final():
    return lax.axis_index("seg") == lax.axis_size("seg") - 1


def finish_kernel(out_before, result, block, precondition, from_first, out, buf, sems):
    @pl.when(at_final())
    def _():
        pre = jnp.transpose(precondition[...])
        copies = []
        for part, span in enumerate(parts_of(result.shape[1])):
            real, imag = product(block[0, span], block[1, span], from_first[0], from_first[1])
            real, imag = weighted(pre[span], real, imag)
            buf[0, span] = result[0, span] + real
            buf[1, span] = result[1, span] + imag
            copy = pltpu.make_async_copy(buf.at[:, span], out.at[:, span], sems.at[part])
            copy.start()
            copies.append(copy)
        for copy in copies:
            copy.wait()


def parts_of(rows):
    step = rows // 3
    return [slice(part * step, (part + 1) * step) for part in range(3)]


def last_kernel(
    near_blocks,
    recv,
    pair,
    matrix,
    interpolation,
    near,
    precondition,
    out,
    result,
    block,
    joined,
    sems,
):
    fetch = pltpu.make_async_copy(near_blocks.at[2], block, sems.at[3])
    pl.when(at_final())(fetch.start)
    pre = jnp.transpose(precondition[...])
    join_four(recv, pair, joined)
    real, imag = product(matrix[0], matrix[1], joined[0], joined[1])
    real, imag = real.astype(BF16), imag.astype(BF16)
    copies = []
    for part, span in enumerate(parts_of(near.shape[1])):
        far_real, far_imag = product(interpolation[0, span], interpolation[1, span], real, imag)
        result[0, span], result[1, span] = weighted(
            pre[span], near[0, span] + far_real, near[1, span] + far_imag
        )
        copy = pltpu.make_async_copy(result.at[:, span], out.at[:, span], sems.at[part])
        copy.start()
        copies.append(copy)
    for copy in copies:
        copy.wait()
    pl.when(at_final())(fetch.wait)


def body(density, near_blocks, projection, transfers, interpolation, precondition):
    rows, angles = density.shape[1:]
    rank = projection.shape[1]
    half = rank // 2
    block = pltpu.VMEM((2, half, angles), BF16)
    whole = pltpu.VMEM((2, rows, angles), F32)
    low16 = pltpu.VMEM((2, rows, angles), BF16)
    square = pltpu.VMEM((2, rank, rank), BF16)
    rows_half = pltpu.VMEM((2, half, rank), BF16)
    low, keep, packed, matrix0, matrix1, matrix2 = call(
        first_kernel,
        4,
        (
            low16,
            block,
            pltpu.VMEM((2, half + rows, angles), BF16),
            pltpu.VMEM((2, rank + half, rank), BF16),
            square,
            square,
        ),
        (density, projection, transfers),
        in_specs=[HBM] * 3,
        scratch=[
            pltpu.VMEM(density.shape, F32),
            pltpu.VMEM(projection.shape, BF16),
            pltpu.SemaphoreType.DMA((7,)),
        ],
    )
    joined = pltpu.VMEM((2, rank, angles), BF16)
    pair = pltpu.VMEM((2, 2, half, rank), BF16)
    packed = swapped(packed, 1)
    keep, send, rows3 = call(
        level0_kernel, 2, (block, block, rows_half), (keep, packed, matrix0), scratch=[joined]
    )
    recv = swapped(send, 2)
    keep, send = call(
        lambda *refs: level_kernel(1, *refs),
        2,
        (block, block),
        (keep, recv, matrix1),
        scratch=[joined],
    )
    recv = swapped(send, 4)
    rows3 = swapped(rows3, 16)
    across = swapped_across(low)
    final = lax.axis_size("seg") - 1
    from_final = moved(low, final, 0)
    from_first = moved(low, 0, final)
    send = call(
        lambda *refs: spread_kernel(2, *refs),
        2,
        jax.ShapeDtypeStruct((4, 2, half, angles), BF16),
        (keep, recv, matrix2),
        out_specs=HBM,
        scratch=[
            joined,
            pltpu.VMEM((2, 2, half, angles), BF16),
            pltpu.SemaphoreType.DMA((4,)),
        ],
    )
    recv = lax.all_to_all(send, "seg", 0, 0, axis_index_groups=groups_of_four(3))
    work = (whole, pltpu.VMEM((2, rows, rank), BF16), pair, square, pltpu.VMEM((2, rows), F32))
    done = ()
    for here in (True, False):
        done = call(
            lambda *refs, here=here: near_kernel(here, *refs),
            6,
            work,
            (
                near_blocks,
                jnp.swapaxes(interpolation, 1, 2),
                transfers,
                precondition,
                low,
                packed,
                rows3,
                from_final if here else across,
                *done,
            ),
            in_specs=[HBM] * 4 + [VMEM] * 2 + [ANY] * 2 + [VMEM] * len(done),
            scratch=[
                pltpu.VMEM(near_blocks.shape, BF16),
                pltpu.VMEM((2, rank, rows), BF16),
                pltpu.VMEM(low.shape, BF16),
                pltpu.SemaphoreType.DMA((9,)),
            ],
            aliases={8 + k: k for k in range(len(done))},
        )
    near, turned, pair, matrix4, scales = done
    out = jax.ShapeDtypeStruct((2, rows, angles), F32)
    out, result, last_block = call(
        last_kernel,
        6,
        (out, whole, pltpu.VMEM(near_blocks.shape[1:], BF16)),
        (near_blocks, recv, pair, matrix4, turned, near, scales),
        in_specs=[HBM] + [VMEM] * 6,
        out_specs=[HBM, VMEM, VMEM],
        scratch=[joined, pltpu.SemaphoreType.DMA((4,))],
    )
    return call(
        finish_kernel,
        4,
        jax.ShapeDtypeStruct((2, rows, angles), F32),
        (out, result, last_block, scales, from_first),
        in_specs=[HBM] + [VMEM] * 4,
        out_specs=HBM,
        scratch=[pltpu.VMEM((2, rows, angles), F32), pltpu.SemaphoreType.DMA((3,))],
        aliases={0: 0},
    )


def solution(mesh):
    placed = (
        P(None, "seg", None),
        P(None, None, "seg", None),
        P(None, "seg", None),
        P(None, None, "seg", None),
        P(None, "seg", None),
        P(None, "seg"),
    )

    return jax.shard_map(
        body, mesh=mesh, in_specs=placed, out_specs=P(None, "seg", None), check_vma=False
    )
```

```python
import jax
import jax.numpy as jnp
from jax import lax
from jax.experimental import pallas as pl
from jax.experimental.pallas import tpu as pltpu
from jax.sharding import PartitionSpec as P


VMEM = pl.BlockSpec(memory_space=pltpu.VMEM)
HBM = pl.BlockSpec(memory_space=pltpu.HBM)
ANY = pl.BlockSpec(memory_space=pl.ANY)
F32 = jnp.float32
BF16 = jnp.bfloat16


def swapped(array, mask):
    return lax.ppermute(array, "seg", [(i, i ^ mask) for i in range(lax.axis_size("seg"))])


def swapped_across(array):
    size = lax.axis_size("seg")
    return lax.ppermute(array, "seg", [(i, ((i + 1) ^ 1) - 1) for i in range(1, size - 1)])


def moved(array, source, target):
    return lax.ppermute(array, "seg", [(source, target)])


def groups_of_four(level):
    low, high = 1 << level, 2 << level
    firsts = [i for i in range(lax.axis_size("seg")) if not i & (low | high)]
    return [[i | low | high, i | high, i | low, i] for i in firsts]


def held(array):
    return pltpu.with_memory_space_constraint(array, pltpu.VMEM)


def in_hbm(array):
    return pltpu.with_memory_space_constraint(array, pltpu.HBM)


PLACE = {pltpu.HBM: in_hbm, pltpu.VMEM: held, pl.ANY: lambda array: array}


def call(kernel, limit, out_shape, operands, in_specs=None, out_specs=None, scratch=(), aliases={}):
    in_specs = in_specs or [VMEM] * len(operands)
    return pl.pallas_call(
        kernel,
        out_shape=out_shape,
        in_specs=in_specs,
        out_specs=out_specs or jax.tree.map(lambda _: VMEM, out_shape),
        scratch_shapes=scratch,
        input_output_aliases=aliases,
        compiler_params=pltpu.CompilerParams(vmem_limit_bytes=limit << 20),
    )(*(PLACE[spec.memory_space](a) for a, spec in zip(operands, in_specs)))


def dot(left, right):
    return jnp.dot(left, right, preferred_element_type=F32)


def bit_of(level):
    return jnp.bitwise_and(jnp.right_shift(lax.axis_index("seg"), level), 1)


def product(real, imag, vec_real, vec_imag):
    return (
        dot(real, vec_real) - dot(imag, vec_imag),
        dot(real, vec_imag) + dot(imag, vec_real),
    )


def store_halves(level, half, matrix, vec_real, vec_imag, keep, send):
    bit = bit_of(level)
    for target, which in ((send, 1 - bit), (keep, bit)):
        rows = pl.ds(pl.multiple_of(which * half, half), half)
        real, imag = product(matrix(0, rows), matrix(1, rows), vec_real, vec_imag)
        target[0] = real.astype(BF16)
        target[1] = imag.astype(BF16)


def join(level, half, keep, recv, joined):
    bit = bit_of(level)
    joined[:, pl.ds(pl.multiple_of(bit * half, half), half)] = keep[...]
    joined[:, pl.ds(pl.multiple_of((1 - bit) * half, half), half)] = recv[...]


def half_rows(which, half):
    return pl.ds(pl.multiple_of(which * half, half), half)


def first_kernel(
    density,
    projection,
    transfers,
    low,
    keep,
    packed,
    matrix0,
    matrix1,
    matrix2,
    dens_buf,
    proj_buf,
    sems,
):
    half = proj_buf.shape[1] // 2
    copies = [
        pltpu.make_async_copy(projection, proj_buf, sems.at[0]),
        pltpu.make_async_copy(density.at[0], dens_buf.at[0], sems.at[1]),
        pltpu.make_async_copy(density.at[1], dens_buf.at[1], sems.at[2]),
        pltpu.make_async_copy(transfers.at[0], matrix0.at[:, 0 : 2 * half], sems.at[3]),
        pltpu.make_async_copy(transfers.at[1], matrix1, sems.at[4]),
        pltpu.make_async_copy(transfers.at[2], matrix2, sems.at[5]),
        pltpu.make_async_copy(transfers.at[3, :, half_rows(1 - bit_of(4), half)], matrix0.at[:, 2 * half :], sems.at[6]),
    ]
    for k in (1, 2, 0, 3, 4, 5, 6):
        copies[k].start()
    for part in range(2):
        copies[part + 1].wait()
        low[part] = dens_buf[part].astype(BF16)
        packed[part, half:] = low[part]
    copies[0].wait()
    store_halves(
        0,
        half,
        lambda part, rows: proj_buf[part, rows],
        low[0],
        low[1],
        keep,
        packed.at[:, 0:half],
    )
    for copy in copies[3:]:
        copy.wait()


def level_kernel(level, keep, recv, matrix, keep_out, send_out, joined):
    half = keep.shape[1]
    join(level, half, keep, recv, joined)
    store_halves(
        level + 1, half, lambda part, rows: matrix[part, rows], joined[0], joined[1], keep_out, send_out
    )


def level0_kernel(keep, recv, matrix, keep_out, send_out, rows3, joined):
    half = keep.shape[1]
    level_kernel(0, keep, recv.at[:, 0:half], matrix, keep_out, send_out, joined)
    rows3[...] = matrix[:, matrix.shape[2] :]


def spread_kernel(level, keep, recv, matrix, out, joined, result, sems):
    half = keep.shape[1]
    join(level, half, keep, recv, joined)
    copies = []
    for which in range(2):
        rows = pl.ds(which * half, half)
        real, imag = product(matrix[0, rows], matrix[1, rows], joined[0], joined[1])
        result[which, 0] = real.astype(BF16)
        result[which, 1] = imag.astype(BF16)
        for member in (1 - which, 3 - which):
            copy = pltpu.make_async_copy(result.at[which], out.at[member], sems.at[member])
            copy.start()
            copies.append(copy)
    for copy in copies:
        copy.wait()


def join_four(recv, pair, joined):
    half = recv.shape[2]
    for side in range(2):
        vecs = [
            jnp.concatenate([recv[3 - 2 * side, part], recv[2 - 2 * side, part]])
            for part in range(2)
        ]
        real, imag = product(pair[side, 0], pair[side, 1], *vecs)
        joined[0, pl.ds(side * half, half)] = real.astype(BF16)
        joined[1, pl.ds(side * half, half)] = imag.astype(BF16)


def near_kernel(here, *refs):
    @pl.when((lax.axis_index("seg") == 0) == here)
    def _():
        near_work(*refs)


def near_work(
    near_blocks,
    interpolation,
    transfers,
    precondition,
    low,
    beside,
    rows3,
    across,
    *refs,
):
    out, turned, pair, matrix4, scales, buf, flat, vec_buf, sems = refs[-9:]
    half = pair.shape[2]
    side = bit_of(4)
    beside = beside.at[:, half:]
    odd = bit_of(0)
    order = ((0, low), (2 - odd, beside), (1 + odd, vec_buf))
    copies = [
        pltpu.make_async_copy(near_blocks.at[block], buf.at[i], sems.at[i])
        for i, (block, _) in enumerate(order)
    ]
    copies += [
        pltpu.make_async_copy(interpolation, flat, sems.at[3]),
        pltpu.make_async_copy(transfers.at[3, :, half_rows(side, half)], pair.at[side], sems.at[4]),
        pltpu.make_async_copy(rows3, pair.at[1 - side], sems.at[7]),
        pltpu.make_async_copy(transfers.at[4], matrix4, sems.at[5]),
        pltpu.make_async_copy(precondition, scales, sems.at[6]),
    ]
    copies.append(pltpu.make_async_copy(across, vec_buf, sems.at[8]))
    for copy in copies:
        copy.start()
    for i, (_, vec) in enumerate(order):
        copies[i].wait()
        if i == 2:
            copies[8].wait()
        real, imag = product(buf[i, 0], buf[i, 1], vec[0], vec[1])
        if i:
            out[0] += real
            out[1] += imag
        else:
            out[0] = real
            out[1] = imag
    for copy in copies[3:8]:
        copy.wait()
    for part in range(2):
        turned[part] = jnp.transpose(flat[part])


def weighted(pre, real, imag):
    return pre[:, 0:1] * real - pre[:, 1:2] * imag, pre[:, 0:1] * imag + pre[:, 1:2] * real


def at_final():
    return lax.axis_index("seg") == lax.axis_size("seg") - 1


def finish_kernel(out_before, result, block, precondition, from_first, out, buf, sems):
    @pl.when(at_final())
    def _():
        pre = jnp.transpose(precondition[...])
        copies = []
        for part, span in enumerate(parts_of(result.shape[1])):
            real, imag = product(block[0, span], block[1, span], from_first[0], from_first[1])
            real, imag = weighted(pre[span], real, imag)
            buf[0, span] = result[0, span] + real
            buf[1, span] = result[1, span] + imag
            copy = pltpu.make_async_copy(buf.at[:, span], out.at[:, span], sems.at[part])
            copy.start()
            copies.append(copy)
        for copy in copies:
            copy.wait()


def parts_of(rows):
    step = rows // 3
    return [slice(part * step, (part + 1) * step) for part in range(3)]


def last_kernel(
    near_blocks,
    recv,
    pair,
    matrix,
    interpolation,
    near,
    precondition,
    out,
    result,
    block,
    joined,
    sems,
):
    fetch = pltpu.make_async_copy(near_blocks.at[2], block, sems.at[3])
    pl.when(at_final())(fetch.start)
    pre = jnp.transpose(precondition[...])
    join_four(recv, pair, joined)
    real, imag = product(matrix[0], matrix[1], joined[0], joined[1])
    real, imag = real.astype(BF16), imag.astype(BF16)
    copies = []
    for part, span in enumerate(parts_of(near.shape[1])):
        far_real, far_imag = product(interpolation[0, span], interpolation[1, span], real, imag)
        result[0, span], result[1, span] = weighted(
            pre[span], near[0, span] + far_real, near[1, span] + far_imag
        )
        copy = pltpu.make_async_copy(result.at[:, span], out.at[:, span], sems.at[part])
        copy.start()
        copies.append(copy)
    for copy in copies:
        copy.wait()
    pl.when(at_final())(fetch.wait)


def body(density, near_blocks, projection, transfers, interpolation, precondition):
    rows, angles = density.shape[1:]
    rank = projection.shape[1]
    half = rank // 2
    block = pltpu.VMEM((2, half, angles), BF16)
    whole = pltpu.VMEM((2, rows, angles), F32)
    low16 = pltpu.VMEM((2, rows, angles), BF16)
    square = pltpu.VMEM((2, rank, rank), BF16)
    rows_half = pltpu.VMEM((2, half, rank), BF16)
    low, keep, packed, matrix0, matrix1, matrix2 = call(
        first_kernel,
        4,
        (
            low16,
            block,
            pltpu.VMEM((2, half + rows, angles), BF16),
            pltpu.VMEM((2, rank + half, rank), BF16),
            square,
            square,
        ),
        (density, projection, transfers),
        in_specs=[HBM] * 3,
        scratch=[
            pltpu.VMEM(density.shape, F32),
            pltpu.VMEM(projection.shape, BF16),
            pltpu.SemaphoreType.DMA((7,)),
        ],
    )
    joined = pltpu.VMEM((2, rank, angles), BF16)
    pair = pltpu.VMEM((2, 2, half, rank), BF16)
    packed = swapped(packed, 1)
    keep, send, rows3 = call(
        level0_kernel, 2, (block, block, rows_half), (keep, packed, matrix0), scratch=[joined]
    )
    recv = swapped(send, 2)
    keep, send = call(
        lambda *refs: level_kernel(1, *refs),
        2,
        (block, block),
        (keep, recv, matrix1),
        scratch=[joined],
    )
    recv = swapped(send, 4)
    rows3 = swapped(rows3, 16)
    across = swapped_across(low)
    final = lax.axis_size("seg") - 1
    from_final = moved(low, final, 0)
    from_first = moved(low, 0, final)
    send = call(
        lambda *refs: spread_kernel(2, *refs),
        2,
        jax.ShapeDtypeStruct((4, 2, half, angles), BF16),
        (keep, recv, matrix2),
        out_specs=HBM,
        scratch=[
            joined,
            pltpu.VMEM((2, 2, half, angles), BF16),
            pltpu.SemaphoreType.DMA((4,)),
        ],
    )
    recv = lax.all_to_all(send, "seg", 0, 0, axis_index_groups=groups_of_four(3))
    work = (whole, pltpu.VMEM((2, rows, rank), BF16), pair, square, pltpu.VMEM((2, rows), F32))
    done = ()
    for here in (True, False):
        done = call(
            lambda *refs, here=here: near_kernel(here, *refs),
            6,
            work,
            (
                near_blocks,
                jnp.swapaxes(interpolation, 1, 2),
                transfers,
                precondition,
                low,
                packed,
                rows3,
                from_final if here else across,
                *done,
            ),
            in_specs=[HBM] * 4 + [VMEM] * 2 + [ANY] * 2 + [VMEM] * len(done),
            scratch=[
                pltpu.VMEM(near_blocks.shape, BF16),
                pltpu.VMEM((2, rank, rows), BF16),
                pltpu.VMEM(low.shape, BF16),
                pltpu.SemaphoreType.DMA((9,)),
            ],
            aliases={8 + k: k for k in range(len(done))},
        )
    near, turned, pair, matrix4, scales = done
    out = jax.ShapeDtypeStruct((2, rows, angles), F32)
    out, result, last_block = call(
        last_kernel,
        6,
        (out, whole, pltpu.VMEM(near_blocks.shape[1:], BF16)),
        (near_blocks, recv, pair, matrix4, turned, near, scales),
        in_specs=[HBM] + [VMEM] * 6,
        out_specs=[HBM, VMEM, VMEM],
        scratch=[joined, pltpu.SemaphoreType.DMA((4,))],
    )
    return call(
        finish_kernel,
        4,
        jax.ShapeDtypeStruct((2, rows, angles), F32),
        (out, result, last_block, scales, from_first),
        in_specs=[HBM] + [VMEM] * 4,
        out_specs=HBM,
        scratch=[pltpu.VMEM((2, rows, angles), F32), pltpu.SemaphoreType.DMA((3,))],
        aliases={0: 0},
    )


def solution(mesh):
    placed = (
        P(None, "seg", None),
        P(None, None, "seg", None),
        P(None, "seg", None),
        P(None, None, "seg", None),
        P(None, "seg", None),
        P(None, "seg"),
    )

    return jax.shard_map(
        body, mesh=mesh, in_specs=placed, out_specs=P(None, "seg", None), check_vma=False
    )
```

```python
import jax
import jax.numpy as jnp
from jax import lax
from jax.experimental import pallas as pl
from jax.experimental.pallas import tpu as pltpu
from jax.sharding import PartitionSpec as P


VMEM = pl.BlockSpec(memory_space=pltpu.VMEM)
HBM = pl.BlockSpec(memory_space=pltpu.HBM)
ANY = pl.BlockSpec(memory_space=pl.ANY)
F32 = jnp.float32
BF16 = jnp.bfloat16


def swapped(array, mask):
    return lax.ppermute(array, "seg", [(i, i ^ mask) for i in range(lax.axis_size("seg"))])


def swapped_across(array):
    size = lax.axis_size("seg")
    return lax.ppermute(array, "seg", [(i, ((i + 1) ^ 1) - 1) for i in range(1, size - 1)])


def moved(array, source, target):
    return lax.ppermute(array, "seg", [(source, target)])


def groups_of_four(level):
    low, high = 1 << level, 2 << level
    firsts = [i for i in range(lax.axis_size("seg")) if not i & (low | high)]
    return [[i | low | high, i | high, i | low, i] for i in firsts]


def held(array):
    return pltpu.with_memory_space_constraint(array, pltpu.VMEM)


def in_hbm(array):
    return pltpu.with_memory_space_constraint(array, pltpu.HBM)


PLACE = {pltpu.HBM: in_hbm, pltpu.VMEM: held, pl.ANY: lambda array: array}


def call(kernel, limit, out_shape, operands, in_specs=None, out_specs=None, scratch=(), aliases={}):
    in_specs = in_specs or [VMEM] * len(operands)
    return pl.pallas_call(
        kernel,
        out_shape=out_shape,
        in_specs=in_specs,
        out_specs=out_specs or jax.tree.map(lambda _: VMEM, out_shape),
        scratch_shapes=scratch,
        input_output_aliases=aliases,
        compiler_params=pltpu.CompilerParams(vmem_limit_bytes=limit << 20),
    )(*(PLACE[spec.memory_space](a) for a, spec in zip(operands, in_specs)))


def dot(left, right):
    return jnp.dot(left, right, preferred_element_type=F32)


def bit_of(level):
    return jnp.bitwise_and(jnp.right_shift(lax.axis_index("seg"), level), 1)


def product(real, imag, vec_real, vec_imag):
    return (
        dot(real, vec_real) - dot(imag, vec_imag),
        dot(real, vec_imag) + dot(imag, vec_real),
    )


def store_halves(level, half, matrix, vec_real, vec_imag, keep, send):
    bit = bit_of(level)
    for target, which in ((send, 1 - bit), (keep, bit)):
        rows = pl.ds(pl.multiple_of(which * half, half), half)
        real, imag = product(matrix(0, rows), matrix(1, rows), vec_real, vec_imag)
        target[0] = real.astype(BF16)
        target[1] = imag.astype(BF16)


def join(level, half, keep, recv, joined):
    bit = bit_of(level)
    joined[:, pl.ds(pl.multiple_of(bit * half, half), half)] = keep[...]
    joined[:, pl.ds(pl.multiple_of((1 - bit) * half, half), half)] = recv[...]


def half_rows(which, half):
    return pl.ds(pl.multiple_of(which * half, half), half)


def first_kernel(
    density,
    projection,
    transfers,
    low,
    keep,
    packed,
    matrix0,
    matrix1,
    matrix2,
    dens_buf,
    proj_buf,
    sems,
):
    half = proj_buf.shape[1] // 2
    copies = [
        pltpu.make_async_copy(projection, proj_buf, sems.at[0]),
        pltpu.make_async_copy(density.at[0], dens_buf.at[0], sems.at[1]),
        pltpu.make_async_copy(density.at[1], dens_buf.at[1], sems.at[2]),
        pltpu.make_async_copy(transfers.at[0], matrix0.at[:, 0 : 2 * half], sems.at[3]),
        pltpu.make_async_copy(transfers.at[1], matrix1, sems.at[4]),
        pltpu.make_async_copy(transfers.at[2], matrix2, sems.at[5]),
        pltpu.make_async_copy(transfers.at[3, :, half_rows(1 - bit_of(4), half)], matrix0.at[:, 2 * half :], sems.at[6]),
    ]
    for k in (1, 2, 0, 3, 4, 5, 6):
        copies[k].start()
    for part in range(2):
        copies[part + 1].wait()
        low[part] = dens_buf[part].astype(BF16)
        packed[part, half:] = low[part]
    copies[0].wait()
    store_halves(
        0,
        half,
        lambda part, rows: proj_buf[part, rows],
        low[0],
        low[1],
        keep,
        packed.at[:, 0:half],
    )
    for copy in copies[3:]:
        copy.wait()


def level_kernel(level, keep, recv, matrix, keep_out, send_out, joined):
    half = keep.shape[1]
    join(level, half, keep, recv, joined)
    store_halves(
        level + 1, half, lambda part, rows: matrix[part, rows], joined[0], joined[1], keep_out, send_out
    )


def level0_kernel(keep, recv, matrix, keep_out, send_out, rows3, joined):
    half = keep.shape[1]
    level_kernel(0, keep, recv.at[:, 0:half], matrix, keep_out, send_out, joined)
    rows3[...] = matrix[:, matrix.shape[2] :]


def spread_kernel(level, keep, recv, matrix, out, joined, result, sems):
    half = keep.shape[1]
    join(level, half, keep, recv, joined)
    copies = []
    for which in range(2):
        rows = pl.ds(which * half, half)
        real, imag = product(matrix[0, rows], matrix[1, rows], joined[0], joined[1])
        result[which, 0] = real.astype(BF16)
        result[which, 1] = imag.astype(BF16)
        for member in (1 - which, 3 - which):
            copy = pltpu.make_async_copy(result.at[which], out.at[member], sems.at[member])
            copy.start()
            copies.append(copy)
    for copy in copies:
        copy.wait()


def join_four(recv, pair, joined):
    half = recv.shape[2]
    for side in range(2):
        vecs = [
            jnp.concatenate([recv[3 - 2 * side, part], recv[2 - 2 * side, part]])
            for part in range(2)
        ]
        real, imag = product(pair[side, 0], pair[side, 1], *vecs)
        joined[0, pl.ds(side * half, half)] = real.astype(BF16)
        joined[1, pl.ds(side * half, half)] = imag.astype(BF16)


def near_kernel(here, *refs):
    @pl.when((lax.axis_index("seg") == 0) == here)
    def _():
        near_work(*refs)


def near_work(
    near_blocks,
    interpolation,
    transfers,
    precondition,
    low,
    beside,
    rows3,
    across,
    *refs,
):
    out, turned, pair, matrix4, scales, buf, flat, vec_buf, sems = refs[-9:]
    half = pair.shape[2]
    side = bit_of(4)
    beside = beside.at[:, half:]
    odd = bit_of(0)
    order = ((0, low), (2 - odd, beside), (1 + odd, vec_buf))
    copies = [
        pltpu.make_async_copy(near_blocks.at[block], buf.at[i], sems.at[i])
        for i, (block, _) in enumerate(order)
    ]
    copies += [
        pltpu.make_async_copy(interpolation, flat, sems.at[3]),
        pltpu.make_async_copy(transfers.at[3, :, half_rows(side, half)], pair.at[side], sems.at[4]),
        pltpu.make_async_copy(rows3, pair.at[1 - side], sems.at[7]),
        pltpu.make_async_copy(transfers.at[4], matrix4, sems.at[5]),
        pltpu.make_async_copy(precondition, scales, sems.at[6]),
    ]
    copies.append(pltpu.make_async_copy(across, vec_buf, sems.at[8]))
    for copy in copies:
        copy.start()
    for i, (_, vec) in enumerate(order):
        copies[i].wait()
        if i == 2:
            copies[8].wait()
        real, imag = product(buf[i, 0], buf[i, 1], vec[0], vec[1])
        if i:
            out[0] += real
            out[1] += imag
        else:
            out[0] = real
            out[1] = imag
    for copy in copies[3:8]:
        copy.wait()
    for part in range(2):
        turned[part] = jnp.transpose(flat[part])


def weighted(pre, real, imag):
    return pre[:, 0:1] * real - pre[:, 1:2] * imag, pre[:, 0:1] * imag + pre[:, 1:2] * real


def at_final():
    return lax.axis_index("seg") == lax.axis_size("seg") - 1


def finish_kernel(out_before, result, block, columns, from_first, out, buf, sems):
    @pl.when(at_final())
    def _():
        copies = []
        for part, span in enumerate(parts_of(result.shape[1])):
            real, imag = product(block[0, span], block[1, span], from_first[0], from_first[1])
            real, imag = weighted(columns[span], real, imag)
            buf[0, span] = result[0, span] + real
            buf[1, span] = result[1, span] + imag
            copy = pltpu.make_async_copy(buf.at[:, span], out.at[:, span], sems.at[part])
            copy.start()
            copies.append(copy)
        for copy in copies:
            copy.wait()


def parts_of(rows):
    step = rows // 3
    return [slice(part * step, (part + 1) * step) for part in range(3)]


def last_kernel(
    near_blocks,
    recv,
    pair,
    matrix,
    interpolation,
    near,
    precondition,
    out,
    result,
    block,
    columns,
    joined,
    sems,
):
    fetch = pltpu.make_async_copy(near_blocks.at[2], block, sems.at[3])
    pl.when(at_final())(fetch.start)
    pre = jnp.transpose(precondition[...])
    join_four(recv, pair, joined)
    real, imag = product(matrix[0], matrix[1], joined[0], joined[1])
    real, imag = real.astype(BF16), imag.astype(BF16)
    copies = []
    for part, span in enumerate(parts_of(near.shape[1])):
        far_real, far_imag = product(interpolation[0, span], interpolation[1, span], real, imag)
        result[0, span], result[1, span] = weighted(
            pre[span], near[0, span] + far_real, near[1, span] + far_imag
        )
        copy = pltpu.make_async_copy(result.at[:, span], out.at[:, span], sems.at[part])
        copy.start()
        copies.append(copy)
    columns[...] = pre
    for copy in copies:
        copy.wait()
    pl.when(at_final())(fetch.wait)


def body(density, near_blocks, projection, transfers, interpolation, precondition):
    rows, angles = density.shape[1:]
    rank = projection.shape[1]
    half = rank // 2
    block = pltpu.VMEM((2, half, angles), BF16)
    whole = pltpu.VMEM((2, rows, angles), F32)
    low16 = pltpu.VMEM((2, rows, angles), BF16)
    square = pltpu.VMEM((2, rank, rank), BF16)
    rows_half = pltpu.VMEM((2, half, rank), BF16)
    low, keep, packed, matrix0, matrix1, matrix2 = call(
        first_kernel,
        4,
        (
            low16,
            block,
            pltpu.VMEM((2, half + rows, angles), BF16),
            pltpu.VMEM((2, rank + half, rank), BF16),
            square,
            square,
        ),
        (density, projection, transfers),
        in_specs=[HBM] * 3,
        scratch=[
            pltpu.VMEM(density.shape, F32),
            pltpu.VMEM(projection.shape, BF16),
            pltpu.SemaphoreType.DMA((7,)),
        ],
    )
    joined = pltpu.VMEM((2, rank, angles), BF16)
    pair = pltpu.VMEM((2, 2, half, rank), BF16)
    packed = swapped(packed, 1)
    keep, send, rows3 = call(
        level0_kernel, 2, (block, block, rows_half), (keep, packed, matrix0), scratch=[joined]
    )
    recv = swapped(send, 2)
    keep, send = call(
        lambda *refs: level_kernel(1, *refs),
        2,
        (block, block),
        (keep, recv, matrix1),
        scratch=[joined],
    )
    recv = swapped(send, 4)
    rows3 = swapped(rows3, 16)
    across = swapped_across(low)
    final = lax.axis_size("seg") - 1
    from_final = moved(low, final, 0)
    from_first = moved(low, 0, final)
    send = call(
        lambda *refs: spread_kernel(2, *refs),
        2,
        jax.ShapeDtypeStruct((4, 2, half, angles), BF16),
        (keep, recv, matrix2),
        out_specs=HBM,
        scratch=[
            joined,
            pltpu.VMEM((2, 2, half, angles), BF16),
            pltpu.SemaphoreType.DMA((4,)),
        ],
    )
    recv = lax.all_to_all(send, "seg", 0, 0, axis_index_groups=groups_of_four(3))
    work = (whole, pltpu.VMEM((2, rows, rank), BF16), pair, square, pltpu.VMEM((2, rows), F32))
    done = ()
    for here in (True, False):
        done = call(
            lambda *refs, here=here: near_kernel(here, *refs),
            6,
            work,
            (
                near_blocks,
                jnp.swapaxes(interpolation, 1, 2),
                transfers,
                precondition,
                low,
                packed,
                rows3,
                from_final if here else across,
                *done,
            ),
            in_specs=[HBM] * 4 + [VMEM] * 2 + [ANY] * 2 + [VMEM] * len(done),
            scratch=[
                pltpu.VMEM(near_blocks.shape, BF16),
                pltpu.VMEM((2, rank, rows), BF16),
                pltpu.VMEM(low.shape, BF16),
                pltpu.SemaphoreType.DMA((9,)),
            ],
            aliases={8 + k: k for k in range(len(done))},
        )
    near, turned, pair, matrix4, scales = done
    out = jax.ShapeDtypeStruct((2, rows, angles), F32)
    out, result, last_block, columns = call(
        last_kernel,
        6,
        (out, whole, pltpu.VMEM(near_blocks.shape[1:], BF16), pltpu.VMEM((rows, 2), F32)),
        (near_blocks, recv, pair, matrix4, turned, near, scales),
        in_specs=[HBM] + [VMEM] * 6,
        out_specs=[HBM, VMEM, VMEM, VMEM],
        scratch=[joined, pltpu.SemaphoreType.DMA((4,))],
    )
    return call(
        finish_kernel,
        4,
        jax.ShapeDtypeStruct((2, rows, angles), F32),
        (out, result, last_block, columns, from_first),
        in_specs=[HBM] + [VMEM] * 4,
        out_specs=HBM,
        scratch=[pltpu.VMEM((2, rows, angles), F32), pltpu.SemaphoreType.DMA((3,))],
        aliases={0: 0},
    )


def solution(mesh):
    placed = (
        P(None, "seg", None),
        P(None, None, "seg", None),
        P(None, "seg", None),
        P(None, None, "seg", None),
        P(None, "seg", None),
        P(None, "seg"),
    )

    return jax.shard_map(
        body, mesh=mesh, in_specs=placed, out_specs=P(None, "seg", None), check_vma=False
    )
```
